32 devices in a mesh: strike: 8 (over y, x, core), dip: 4 (over z).
Axes of the slice: x: 2, y: 2, z: 4, core: 2. Of those that a mesh axis runs over, the one named last changes fastest.
Arguments:
- adjoint_state: float32 [9, 64, 64, 128], P(None, 'strike', 'dip'), may hold values from -6 to 6
- lame_lambda: float32 [64, 64, 128], P('strike', 'dip'), may hold values from 0.5 to 2
- lame_mu: float32 [64, 64, 128], P('strike', 'dip'), may hold values from 0.3 to 1.5
- buoyancy: float32 [64, 64, 128], P('strike', 'dip'), may hold values from 0.5 to 2
- residual: bfloat16 [16384, 3, 128], P(('strike', 'dip')), may hold values from -6 to 6
- receiver_tile: int32 [16384, 1], P(('strike', 'dip')), may hold values from 0 to 31; in each aligned block of 512 rows (0 to 511, 512 to 1023, ...) at most 32 rows name the same one
- receiver_cell: int32 [16384], P(('strike', 'dip')), may hold values from 0 to 16383, as said below
- resample: float32 [2, 128], replicated, may hold values from -0.5 to 0.5
- fault_patch: int32 [32, 256], P(('strike', 'dip')), may hold values from 0 to 2047, as said below
- fault_cell: int32 [32, 256], P(('strike', 'dip')), may hold values from 0 to 16383, as said below
- fault_area: float32 [32, 256], P(('strike', 'dip')), may hold values from 0.25 to 1
- moment: float32 [6, 2048], replicated, may hold values from -6 to 6
- subpatch_order: int32 [2048], replicated, may hold values from 0 to 2047, each once
Outputs:
- adjoint_out: float32 [9, 64, 64, 128], P(None, 'strike', 'dip')
- slip_gradient: float32 [2, 2048], P(None, ('strike', 'dip'))
The draws below stay inside these ranges and needn't reach their ends.
Inputs may be any that keep to these rules, and one draw needn't show every extreme that they name: `receiver_tile`: tile t is the device at index t of strike+dip. In the rows of one device at most 32 stations name the same tile. `receiver_cell`: cell of the station within the block of tile receiver_tile. `fault_patch`: the entries of tile t name subpatches within 132 of t * 64, counted cyclically. `fault_cell`: cell of the entry within the block of the tile of its row.
All inputs are finite; a program needn't handle non-finite values.
Results may differ from the reference program's by a relative error of at most 0.0003.
Values may be sent and summed in bfloat16 or wider, within the bound.
A program may use at most 64 MiB of HBM per device.

```python
import math
import jax
import jax.numpy as jnp
import numpy as np
from jax import lax

CX = 8
CY = 16
CZ = 128
STEPS = 2
NT = 128
REC_DEV = 512
SUBPATCHES = 2048
FENT = 256
TILES = 32
NX = 64
NY = 64
NZ = 128
STATIONS = 16384
SLOT = 32
SUB_OWN = 64
N_DIP = 4


def spread_cells(key, entry_count):
    cell_total = CX * CY * CZ
    values = jax.random.randint(key, (entry_count,), 0, cell_total, dtype=jnp.int32)
    anchor = jax.random.randint(jax.random.fold_in(key, 7), (), 0, entry_count, dtype=jnp.int32)
    values = values.at[anchor].set(0)
    values = values.at[(anchor + 1) % entry_count].set(cell_total - 1)
    return values


def draw_receiver_cell(key, part):
    return spread_cells(jax.random.fold_in(key, 5), STATIONS)


def draw_fault_cell(key, part):
    return spread_cells(jax.random.fold_in(key, 11), TILES * FENT).reshape(TILES, FENT)


def draw_fault_patch(key, part):
    id_spread = 2 * SUB_OWN + 4
    starts = jnp.arange(TILES, dtype=jnp.int32) * SUB_OWN
    offsets = jax.random.randint(jax.random.fold_in(key, 3), (TILES, FENT), -id_spread, id_spread + 1, dtype=jnp.int32)
    patches = (starts[:, None] + offsets) % SUBPATCHES
    patches = patches.at[:, 0].set(starts + SUB_OWN - 1)
    patches = patches.at[:, 1].set(starts)
    return patches.astype(jnp.int32)


def shard_levels(stream_key, shape, cuts, smallest, largest):
    loudness = 1.0
    for axis_at, parts in cuts:
        heights = jax.random.uniform(jax.random.fold_in(jax.random.fold_in(stream_key, 6), axis_at), (parts,), jnp.float32, smallest / len(cuts), largest / len(cuts))
        loudness = loudness * jnp.repeat(jnp.exp(heights), shape[axis_at] // parts).reshape((-1,) + (1,) * (len(shape) - 1 - axis_at))
    return loudness


def routed_block(key, own, number, rows, count, top, reach, skew):
    sequence = jax.random.permutation(key, count)
    packed, common = shares(count, rows * top, reach, skew, True), shares(count, rows * top, reach, skew, False)
    places = jnp.arange(count)

    def named(lengths, rotation):
        used = int((lengths > 0).sum())
        fixed = max(1, used // 4)
        passed = fixed + (places - fixed + rotation * (used - fixed)) % max(1, count - fixed)
        return jnp.zeros((count,), jnp.int32).at[sequence[jnp.where(places < fixed, places, passed)]].set(jnp.asarray(lengths, jnp.int32))

    lengths = jnp.where(number % 4 == 0, named(packed, number // 4), named(common, number - number // 4 - 1))
    mixed = jax.random.permutation(jax.random.fold_in(own, 3), count)
    source_of, sink = mixed[0:count // 2 * 2:2], mixed[1:count // 2 * 2:2]
    margin = jnp.minimum(lengths[source_of] - 1, reach - lengths[sink]) // 2
    margin = jnp.where((source_of == sequence[0]) | (sink == sequence[0]) | (lengths[sink] == 0), 0, jnp.maximum(margin, 0))
    passed = jax.random.randint(jax.random.fold_in(own, 4), (count // 2,), 0, 1 << 20) % (margin + 1)
    lengths = lengths.at[source_of].add(-passed).at[sink].add(passed)
    members = jnp.searchsorted(jnp.cumsum(lengths), jnp.arange(rows * top), side="right").astype(jnp.int32)
    table = members.reshape(top, rows).T
    table = table[jax.random.permutation(jax.random.fold_in(own, 1), rows)]
    rotation = jax.random.randint(jax.random.fold_in(own, 2), (rows, 1), 0, top)
    return jnp.take_along_axis(table, (jnp.arange(top)[None, :] + rotation) % top, axis=1)


def shares(amount, total, bound, slope, full):
    weights = [(1 << 20) // math.isqrt(rank ** slope) + 1 for rank in range(1, amount + 1)]
    largest = bound if full else min(bound, max(-(-total // amount), total * weights[0] // sum(weights)))
    least = 1 if total - largest >= amount - 1 else 0
    given, rest = [largest] + [least] * (amount - 1), total - largest - least * (amount - 1)
    while rest > 0:
        free = [i for i in range(1, amount) if given[i] < largest] or [i for i in range(1, amount) if given[i] < bound]
        whole, left = sum([weights[i] for i in free]), rest
        for i in free:
            more = min(bound - given[i], max(1, left * weights[i] // whole), rest)
            given[i] = given[i] + more
            rest = rest - more
    return np.array(given)


def normal_values(stream_key, shape, width, reach, shards=(), held_as=jnp.bfloat16):
    values = width * jax.random.normal(stream_key, shape, jnp.float32)
    if shards:
        values = values * shard_levels(stream_key, shape, shards, -0.22, 0.18)
    return jnp.clip(values, -reach, reach).astype(held_as)


def setup_inputs(seed: int = 0) -> dict:
    seeds = jax.random.split(jax.random.key(seed), 14)
    adjoint_state = normal_values(seeds[0], (9, NX, NY, NZ), 1.0, 6.0, ((1, 8), (2, 4)), jnp.float32)
    lame_lambda = jnp.clip(jnp.exp(math.log(2.0) - 1.3862944 * jax.random.uniform(seeds[1], (NX, NY, NZ), jnp.float32) ** shard_levels(seeds[1], (NX, NY, NZ), ((0, 8), (1, 4)), -0.2, 0.2)), 0.5, 2.0)
    lame_mu = jnp.clip(jnp.exp(math.log(1.5) - 1.60943787 * jax.random.uniform(seeds[2], (NX, NY, NZ), jnp.float32) ** shard_levels(seeds[2], (NX, NY, NZ), ((0, 8), (1, 4)), -0.2, 0.2)), 0.3, 1.5)
    buoyancy = jnp.clip(jnp.exp(math.log(2.0) - 1.3862944 * jax.random.uniform(seeds[3], (NX, NY, NZ), jnp.float32) ** shard_levels(seeds[3], (NX, NY, NZ), ((0, 8), (1, 4)), -0.2, 0.2)), 0.5, 2.0)
    residual = normal_values(seeds[4], (STATIONS, 3, NT), 1.0, 6.0, ((0, 32),))
    receiver_tile_keys = jax.random.split(jax.random.fold_in(seeds[5], 1), STATIONS // REC_DEV)
    receiver_tile_turns = jax.random.permutation(jax.random.fold_in(seeds[5], 3), STATIONS // REC_DEV)
    receiver_tile = jax.vmap(lambda own, number: routed_block(jax.random.fold_in(seeds[5], 2), own, number, REC_DEV, TILES, 1, SLOT, 2))(receiver_tile_keys, receiver_tile_turns).reshape((STATIONS, 1))
    receiver_cell = draw_receiver_cell(jax.random.fold_in(seeds[13], 71), 0)
    resample = normal_values(seeds[7], (STEPS, NT), NT ** -0.5, 0.5, (), jnp.float32)
    fault_patch = draw_fault_patch(jax.random.fold_in(seeds[13], 71), 0)
    fault_cell = draw_fault_cell(jax.random.fold_in(seeds[13], 71), 0)
    fault_area = jnp.clip(jnp.exp(math.log(1.0) - 1.3862944 * jax.random.uniform(seeds[10], (TILES, FENT), jnp.float32) ** shard_levels(seeds[10], (TILES, FENT), ((0, 32),), -0.2, 0.2)), 0.25, 1.0)
    moment = normal_values(seeds[11], (6, SUBPATCHES), 1.0, 6.0, (), jnp.float32)
    subpatch_order = jax.random.permutation(seeds[12], SUBPATCHES).astype(jnp.int32)
    return dict(adjoint_state=adjoint_state, lame_lambda=lame_lambda, lame_mu=lame_mu, buoyancy=buoyancy, residual=residual, receiver_tile=receiver_tile, receiver_cell=receiver_cell, resample=resample, fault_patch=fault_patch, fault_cell=fault_cell, fault_area=fault_area, moment=moment, subpatch_order=subpatch_order)


time_step = 0.25


def derivatives(padded):
    along_x = (padded[:, 2:, 1:-1, 1:-1] - padded[:, :-2, 1:-1, 1:-1]) * 0.5
    along_y = (padded[:, 1:-1, 2:, 1:-1] - padded[:, 1:-1, :-2, 1:-1]) * 0.5
    along_z = (padded[:, 1:-1, 1:-1, 2:] - padded[:, 1:-1, 1:-1, :-2]) * 0.5
    return along_x, along_y, along_z


def velocity_update(velocity, stress_padded, source, buoyancy):
    along_x, along_y, along_z = derivatives(stress_padded)
    force_x = along_x[0] + along_y[3] + along_z[4]
    force_y = along_x[3] + along_y[1] + along_z[5]
    force_z = along_x[4] + along_y[5] + along_z[2]
    return velocity + time_step * (buoyancy * jnp.stack([force_x, force_y, force_z]) + source)


def stress_update(stress, velocity_padded, lame_lambda, lame_mu):
    along_x, along_y, along_z = derivatives(velocity_padded)
    dilation = along_x[0] + along_y[1] + along_z[2]
    return jnp.stack([
        stress[0] + time_step * (lame_lambda * dilation + 2.0 * lame_mu * along_x[0]),
        stress[1] + time_step * (lame_lambda * dilation + 2.0 * lame_mu * along_y[1]),
        stress[2] + time_step * (lame_lambda * dilation + 2.0 * lame_mu * along_z[2]),
        stress[3] + time_step * lame_mu * (along_y[0] + along_x[1]),
        stress[4] + time_step * lame_mu * (along_z[0] + along_x[2]),
        stress[5] + time_step * lame_mu * (along_z[1] + along_y[2]),
    ])


def pad_cells(field):
    return jnp.pad(field, ((0, 0), (1, 1), (1, 1), (1, 1)))


def global_cells(tile_ids, offsets):
    strike_tile = tile_ids // N_DIP
    dip_tile = tile_ids % N_DIP
    coord_x = (strike_tile * CX + offsets // (CY * CZ)).astype(jnp.int32)
    coord_y = (dip_tile * CY + (offsets // CZ) % CY).astype(jnp.int32)
    coord_z = (offsets % CZ).astype(jnp.int32)
    return coord_x, coord_y, coord_z


def reference(adjoint_state, lame_lambda, lame_mu, buoyancy, residual, receiver_tile, receiver_cell, resample, fault_patch, fault_cell, fault_area, moment, subpatch_order):
    velocity = adjoint_state[0:3]
    stress = adjoint_state[3:9]
    amplitude = jnp.einsum("rct,kt->krc", residual.astype(jnp.float32), resample, precision=lax.Precision.HIGHEST)
    station_x, station_y, station_z = global_cells(receiver_tile[:, 0], receiver_cell)
    tile_ids = jnp.repeat(jnp.arange(TILES, dtype=jnp.int32), FENT)
    fault_x, fault_y, fault_z = global_cells(tile_ids, fault_cell.reshape(-1))
    patch_ids = fault_patch.reshape(-1)
    areas = fault_area.reshape(-1)
    pattern = moment[:, patch_ids]
    results = []
    for step in range(STEPS):
        source = jnp.zeros((3, NX, NY, NZ), jnp.float32).at[:, station_x, station_y, station_z].add(amplitude[step].T)
        velocity = velocity_update(velocity, pad_cells(stress), source, buoyancy)
        stress = stress_update(stress, pad_cells(velocity), lame_lambda, lame_mu)
        sampled = stress[:, fault_x, fault_y, fault_z]
        contrib = areas * jnp.sum(pattern * sampled, axis=0)
        partial_sum = jnp.zeros((SUBPATCHES,), jnp.float32).at[patch_ids].add(contrib)
        results.append(partial_sum[subpatch_order])
    return jnp.concatenate([velocity, stress]), jnp.stack(results)
```

```python
import functools

import jax
import jax.numpy as jnp
from jax import lax
from jax.experimental import pallas as pl
from jax.experimental.pallas import tpu as pltpu
from jax.sharding import PartitionSpec as P

STEPS = 2
LANES = 128

time_step = 0.25

MESH = pl.DeviceIdType.MESH
NT_DIMS = (((1,), (1,)), ((), ()))


def split(x):
    high = x.astype(jnp.bfloat16)
    return high, (x - high.astype(jnp.float32)).astype(jnp.bfloat16)


def one_hot(shape, axis, ids):
    return jnp.where(lax.broadcasted_iota(jnp.int32, shape, axis) == ids, 1.0, 0.0).astype(jnp.bfloat16)


def matmul(a, b):
    return jnp.dot(a, b, preferred_element_type=jnp.float32)


def matmul_nt(a, b):
    return lax.dot_general(a, b, NT_DIMS, preferred_element_type=jnp.float32)


def along_x(f, low, high):
    before = jnp.concatenate([low[None], f[:-1]], axis=0)
    after = jnp.concatenate([f[1:], high[None]], axis=0)
    return (after - before) * 0.5


def along_y(f, low, high):
    size = f.shape[1]
    at = lax.broadcasted_iota(jnp.int32, f.shape, 1)
    before = jnp.where(at == 0, low, pltpu.roll(f, 1, 1))
    after = jnp.where(at == size - 1, high, pltpu.roll(f, size - 1, 1))
    return (after - before) * 0.5


def along_z(f):
    size = f.shape[2]
    at = lax.broadcasted_iota(jnp.int32, f.shape, 2)
    before = jnp.where(at == 0, 0.0, pltpu.roll(f, 1, 2))
    after = jnp.where(at == size - 1, 0.0, pltpu.roll(f, size - 1, 2))
    return (after - before) * 0.5


def kernel(
    strike_count,
    dip_count,
    slot_count,
    state,
    lam,
    mu,
    buoy,
    residual,
    tiles,
    cells,
    resample,
    patch,
    fault_cell,
    area,
    moment,
    order,
    out,
    slip,
    packed,
    landed,
    source,
    onehot_hi,
    picks,
    sums_out,
    sums_in,
    x_out,
    x_low,
    x_high,
    y_out,
    y_low,
    y_high,
    route_send,
    route_recv,
    sum_send,
    sum_recv,
    halo_send,
    halo_recv,
):
    count = strike_count * dip_count
    strike = lax.axis_index("strike")
    dip = lax.axis_index("dip")
    me = strike * dip_count + dip
    size_x, size_y, size_z = buoy.shape
    rows = size_x * size_y
    stations = residual.shape[1]
    steps = resample.shape[0]
    shift = size_z.bit_length() - 1
    slots = count * slot_count
    groups = slots // LANES
    per_group = LANES // slot_count
    owned = order.shape[1] // count
    per_block = LANES // owned
    blocks = order.shape[1] // LANES

    def peer(k):
        to = lax.rem(me + k, count)
        return to, (to // dip_count, lax.rem(to, dip_count))

    barrier = pltpu.get_barrier_semaphore()

    def greet(k, carry):
        _, device = peer(k)
        pl.semaphore_signal(barrier, inc=1, device_id=device, device_id_type=MESH)
        return carry

    lax.fori_loop(1, count, greet, 0)

    sides = (
        (strike > 0, (strike - 1, dip)),
        (strike < strike_count - 1, (strike + 1, dip)),
        (dip > 0, (strike, dip - 1)),
        (dip < dip_count - 1, (strike, dip + 1)),
    )
    halves = ((x_out, x_low, x_high), (y_out, y_low, y_high))

    def halo_copies(turn):
        copies = []
        for side in range(4):
            sender, low, high = halves[side // 2]
            target = high if side % 2 == 0 else low
            arrival = side ^ 1
            copies.append(
                pltpu.make_async_remote_copy(
                    src_ref=sender.at[turn, side % 2],
                    dst_ref=target.at[turn],
                    send_sem=halo_send.at[turn, side],
                    recv_sem=halo_recv.at[turn, arrival],
                    device_id=sides[side][1],
                    device_id_type=MESH,
                )
            )
        return copies

    def stage(turn, x_fields, y_fields):
        for c in range(3):
            f = out[x_fields[c]] if turn else state[x_fields[c]]
            x_out[turn, 0, c] = f[0]
            x_out[turn, 1, c] = f[size_x - 1]
            f = out[y_fields[c]] if turn else state[y_fields[c]]
            y_out[turn, 0, c] = f[:, 0:1]
            y_out[turn, 1, c] = f[:, size_y - 1 : size_y]

    def send(turn):
        for side, copy in enumerate(halo_copies(turn)):
            pl.when(sides[side][0])(copy.start)

    def receive(turn):
        for side, copy in enumerate(halo_copies(turn)):

            def finish(turn=turn, side=side, copy=copy):
                copy.wait_send()
                sender, low, high = halves[side // 2]
                target = low if side % 2 == 0 else high
                pltpu.make_async_copy(target.at[turn], target.at[turn], halo_recv.at[turn, side]).wait()

            pl.when(sides[side][0])(finish)

    for side in range(4):

        def clear(side=side):
            _, low, high = halves[side // 2]
            target = low if side % 2 == 0 else high
            target[...] = jnp.zeros_like(target)

        pl.when(jnp.logical_not(sides[side][0]))(clear)

    stress_x, stress_y = (3, 6, 7), (6, 4, 8)
    stage(0, stress_x, stress_y)

    res_hi, res_lo = split(resample[...])
    weights = jnp.concatenate([res_hi, res_lo], axis=0)
    parts = [matmul_nt(weights, residual[c]) for c in range(3)]
    amplitude = [parts[c][k : k + 1] + parts[c][steps + k : steps + k + 1] for k in range(steps) for c in range(3)]
    cell_row = cells[...]
    hi_row = lax.shift_right_logical(cell_row, shift).astype(jnp.float32)
    lo_row = (cell_row & (size_z - 1)).astype(jnp.float32)
    values = jnp.concatenate(amplitude + [hi_row, lo_row], axis=0)
    tile_row = tiles[...]
    named = one_hot((count, stations), 0, tile_row)
    earlier = jnp.where(
        lax.broadcasted_iota(jnp.int32, (stations, stations), 0) < lax.broadcasted_iota(jnp.int32, (stations, stations), 1),
        1.0,
        0.0,
    ).astype(jnp.bfloat16)
    ordinal = jnp.sum(named.astype(jnp.float32) * matmul(named, earlier), axis=0, keepdims=True)
    slot_row = tile_row * slot_count + ordinal.astype(jnp.int32)
    placing = one_hot((slots, stations), 0, slot_row)
    val_hi, val_lo = split(values)
    placed = matmul_nt(jnp.concatenate([val_hi, val_lo], axis=0), placing)
    placed = placed[:8] + placed[8:]
    for g in range(groups):
        packed[g] = placed[:, g * LANES : (g + 1) * LANES]

    pl.semaphore_wait(barrier, count - 1)
    send(0)

    def route(k, carry):
        to, device = peer(k)
        pltpu.make_async_remote_copy(
            src_ref=packed.at[to // per_group],
            dst_ref=landed.at[me],
            send_sem=route_send,
            recv_sem=route_recv,
            device_id=device,
            device_id_type=MESH,
        ).start()
        return carry

    lax.fori_loop(1, count, route, 0)
    landed[me] = packed[me // per_group]

    patch_row = patch[...]
    entries = patch_row.shape[1]
    cell_e = fault_cell[...]
    pick_lo = one_hot((size_z, entries), 0, cell_e & (size_z - 1))
    onehot_hi[...] = jnp.where(
        lax.broadcasted_iota(jnp.int32, (rows, entries), 0) == lax.shift_right_logical(cell_e, shift), 1.0, 0.0
    )
    mom_hi, mom_lo = split(moment[...])
    chosen = matmul(jnp.concatenate([mom_hi, mom_lo], axis=0), one_hot((moment.shape[1], entries), 0, patch_row))
    pattern = (chosen[:6] + chosen[6:]) * area[...]
    patch_col = jnp.transpose(jnp.broadcast_to(patch_row.astype(jnp.float32), (LANES, entries)))
    for b in range(blocks):
        ids = order[:, b * LANES : (b + 1) * LANES].astype(jnp.float32)
        picks[:, b * LANES : (b + 1) * LANES] = jnp.where(patch_col == ids, 1.0, 0.0).astype(jnp.bfloat16)

    def force(turn, c, fields):
        xx, yy, zz = fields
        fx = (out if turn else state)[xx]
        fy = (out if turn else state)[yy]
        fz = (out if turn else state)[zz]
        total = along_x(fx, x_low[turn, c], x_high[turn, c]) + along_y(fy, y_low[turn, c], y_high[turn, c]) + along_z(fz)
        return time_step * (buoy[...] * total)

    rhs = ((3, 6, 7), (6, 4, 8), (7, 8, 5))

    def velocity(turn, step):
        for c in range(3):
            old = (out if turn else state)[c]
            moved = old + force(turn, c, rhs[c])
            if step:
                moved = moved + time_step * source[step * 3 + c].reshape(size_x, size_y, size_z)
            out[c] = moved

    def stress(turn, first):
        old = state if first else out
        lam_v, mu_v = lam[...], mu[...]
        vx, vy, vz = out[0], out[1], out[2]
        dxx = along_x(vx, x_low[turn, 0], x_high[turn, 0])
        dyy = along_y(vy, y_low[turn, 1], y_high[turn, 1])
        dzz = along_z(vz)
        bulk = lam_v * (dxx + dyy + dzz)
        out[3] = old[3] + time_step * (bulk + 2.0 * mu_v * dxx)
        out[4] = old[4] + time_step * (bulk + 2.0 * mu_v * dyy)
        out[5] = old[5] + time_step * (bulk + 2.0 * mu_v * dzz)
        scaled = time_step * mu_v
        out[6] = old[6] + scaled * (
            along_y(vx, y_low[turn, 0], y_high[turn, 0]) + along_x(vy, x_low[turn, 1], x_high[turn, 1])
        )
        out[7] = old[7] + scaled * (along_z(vx) + along_x(vz, x_low[turn, 2], x_high[turn, 2]))
        out[8] = old[8] + scaled * (along_z(vy) + along_y(vz, y_low[turn, 2], y_high[turn, 2]))

    def contribution():
        total = None
        for m in range(6):
            high, low = split(out[3 + m].reshape(rows, size_z))
            taken = (matmul(high, pick_lo) + matmul(low, pick_lo)) * pattern[m : m + 1]
            total = taken if total is None else total + taken
        return jnp.sum(total * onehot_hi[...], axis=0, keepdims=True)

    receive(0)
    velocity(0, 0)

    all_landed = landed.at[pl.ds(0, count - 1)]
    pltpu.make_async_copy(all_landed, all_landed, route_recv).wait()
    pltpu.make_async_copy(all_landed, all_landed, route_send).wait()
    mine = lax.rem(me, per_group)
    lane = lax.broadcasted_iota(jnp.int32, (8, LANES), 1)
    gathered = []
    for g in range(groups):
        total = jnp.zeros((8, LANES), jnp.float32)
        for j in range(per_group):
            turned = pltpu.roll(landed[g * per_group + j], lax.rem(j - mine + per_group, per_group) * slot_count, 1)
            total = jnp.where(lane // slot_count == j, turned, total)
        gathered.append(total)
    arrived = jnp.concatenate(gathered, axis=1)
    hi_ids = arrived[6:7].astype(jnp.int32)
    lo_ids = arrived[7:8].astype(jnp.int32)
    spread_lo = one_hot((size_z, slots), 0, lo_ids)
    row_mask = lax.broadcasted_iota(jnp.int32, (rows, slots), 0) == hi_ids
    amp_hi, amp_lo = split(arrived)
    amp_hi, amp_lo = amp_hi.astype(jnp.float32), amp_lo.astype(jnp.float32)
    for m in range(steps * 3):
        high = jnp.where(row_mask, amp_hi[m : m + 1], 0.0).astype(jnp.bfloat16)
        low = jnp.where(row_mask, amp_lo[m : m + 1], 0.0).astype(jnp.bfloat16)
        source[m] = matmul_nt(high, spread_lo) + matmul_nt(low, spread_lo)
    for c in range(3):
        out[c] = out[c] + time_step * source[c].reshape(size_x, size_y, size_z)

    flow = (0, 1, 2)
    contribs = []
    for step in range(steps):
        if step:
            receive(2 * step)
            velocity(2 * step, step)
        stage(2 * step + 1, flow, flow)
        send(2 * step + 1)
        receive(2 * step + 1)
        stress(2 * step + 1, step == 0)
        if step < steps - 1:
            stage(2 * step + 2, stress_x, stress_y)
            send(2 * step + 2)
        contribs.append(contribution())

    con_hi, con_lo = split(jnp.concatenate(contribs, axis=0))
    summed = matmul(jnp.concatenate([con_hi, con_lo], axis=0), picks[...])
    summed = summed[:steps] + summed[steps:]
    for b in range(blocks):
        sums_out[b] = summed[:, b * LANES : (b + 1) * LANES]

    def spread(k, carry):
        to, device = peer(k)
        pltpu.make_async_remote_copy(
            src_ref=sums_out.at[to // per_block],
            dst_ref=sums_in.at[me],
            send_sem=sum_send,
            recv_sem=sum_recv,
            device_id=device,
            device_id_type=MESH,
        ).start()
        return carry

    lax.fori_loop(1, count, spread, 0)
    sums_in[me] = sums_out[me // per_block]
    all_sums = sums_in.at[pl.ds(0, count - 1)]
    pltpu.make_async_copy(all_sums, all_sums, sum_recv).wait()
    pltpu.make_async_copy(all_sums, all_sums, sum_send).wait()
    final = jnp.sum(sums_in[...], axis=0)
    final = jnp.concatenate([final, jnp.zeros((8 - steps, LANES), jnp.float32)], axis=0)
    first = lax.rem(me, per_block) * owned
    slip[...] = pltpu.roll(final, lax.rem(LANES - first, LANES), 1)[:steps, :owned]


def shards(
    adjoint_state,
    lame_lambda,
    lame_mu,
    buoyancy,
    residual,
    receiver_tile,
    receiver_cell,
    resample,
    fault_patch,
    fault_cell,
    fault_area,
    moment,
    subpatch_order,
):
    strike_count = lax.axis_size("strike")
    dip_count = lax.axis_size("dip")
    count = strike_count * dip_count
    stations = residual.shape[0]
    slot_count = max(2, (2 * stations + count - 1) // count)
    steps = resample.shape[0]
    size_x, size_y, size_z = buoyancy.shape
    rows = size_x * size_y
    slots = count * slot_count
    entries = fault_patch.shape[1]
    patches = moment.shape[1]
    turns = 2 * steps
    vmem = pl.BlockSpec(memory_space=pltpu.VMEM)
    f32, bf16 = jnp.float32, jnp.bfloat16
    return pl.pallas_call(
        functools.partial(kernel, strike_count, dip_count, slot_count),
        out_shape=(
            jax.ShapeDtypeStruct(adjoint_state.shape, f32),
            jax.ShapeDtypeStruct((steps, patches // count), f32),
        ),
        in_specs=[vmem] * 13,
        out_specs=(vmem, vmem),
        scratch_shapes=[
            pltpu.VMEM((slots // LANES, 8, LANES), f32),
            pltpu.VMEM((count, 8, LANES), f32),
            pltpu.VMEM((steps * 3, rows, size_z), f32),
            pltpu.VMEM((rows, entries), f32),
            pltpu.VMEM((entries, patches), bf16),
            pltpu.VMEM((patches // LANES, steps, LANES), f32),
            pltpu.VMEM((count, steps, LANES), f32),
            pltpu.VMEM((turns, 2, 3, size_y, size_z), f32),
            pltpu.VMEM((turns, 3, size_y, size_z), f32),
            pltpu.VMEM((turns, 3, size_y, size_z), f32),
            pltpu.VMEM((turns, 2, 3, size_x, 1, size_z), f32),
            pltpu.VMEM((turns, 3, size_x, 1, size_z), f32),
            pltpu.VMEM((turns, 3, size_x, 1, size_z), f32),
            pltpu.SemaphoreType.DMA,
            pltpu.SemaphoreType.DMA,
            pltpu.SemaphoreType.DMA,
            pltpu.SemaphoreType.DMA,
            pltpu.SemaphoreType.DMA((turns, 4)),
            pltpu.SemaphoreType.DMA((turns, 4)),
        ],
        compiler_params=pltpu.CompilerParams(collective_id=0, has_side_effects=True),
        name="adjoint",
    )(
        adjoint_state,
        lame_lambda,
        lame_mu,
        buoyancy,
        jnp.swapaxes(residual, 0, 1),
        receiver_tile.reshape(1, stations),
        receiver_cell.reshape(1, stations),
        resample,
        fault_patch,
        fault_cell,
        fault_area,
        moment,
        subpatch_order.reshape(1, -1),
    )


def solution(mesh):
    return jax.shard_map(
        shards,
        mesh=mesh,
        in_specs=(
            P(None, "strike", "dip", None),
            P("strike", "dip", None),
            P("strike", "dip", None),
            P("strike", "dip", None),
            P(("strike", "dip"), None, None),
            P(("strike", "dip"), None),
            P(("strike", "dip")),
            P(),
            P(("strike", "dip"), None),
            P(("strike", "dip"), None),
            P(("strike", "dip"), None),
            P(),
            P(),
        ),
        out_specs=(P(None, "strike", "dip", None), P(None, ("strike", "dip"))),
        check_vma=False,
    )
```

```python
import functools

import jax
import jax.numpy as jnp
from jax import lax
from jax.experimental import pallas as pl
from jax.experimental.pallas import tpu as pltpu
from jax.sharding import PartitionSpec as P

STEPS = 2
LANES = 128

time_step = 0.25

MESH = pl.DeviceIdType.MESH
NT_DIMS = (((1,), (1,)), ((), ()))


def split(x):
    high = x.astype(jnp.bfloat16)
    return high, (x - high.astype(jnp.float32)).astype(jnp.bfloat16)


def one_hot(shape, axis, ids):
    return jnp.where(lax.broadcasted_iota(jnp.int32, shape, axis) == ids, 1.0, 0.0).astype(jnp.bfloat16)


def matmul(a, b):
    return jnp.dot(a, b, preferred_element_type=jnp.float32)


def matmul_nt(a, b):
    return lax.dot_general(a, b, NT_DIMS, preferred_element_type=jnp.float32)


def along_x(f, low, high):
    before = jnp.concatenate([low[None], f[:-1]], axis=0)
    after = jnp.concatenate([f[1:], high[None]], axis=0)
    return (after - before) * 0.5


def along_y(f, low, high):
    size = f.shape[1]
    at = lax.broadcasted_iota(jnp.int32, f.shape, 1)
    before = jnp.where(at == 0, low, pltpu.roll(f, 1, 1))
    after = jnp.where(at == size - 1, high, pltpu.roll(f, size - 1, 1))
    return (after - before) * 0.5


def along_z(f):
    size = f.shape[2]
    at = lax.broadcasted_iota(jnp.int32, f.shape, 2)
    before = jnp.where(at == 0, 0.0, pltpu.roll(f, 1, 2))
    after = jnp.where(at == size - 1, 0.0, pltpu.roll(f, size - 1, 2))
    return (after - before) * 0.5


def kernel(strike_count, dip_count, slot_count, *refs):
    (far, refs) = (refs[:13], refs[13:])
    (out, slip), refs = refs[:2], refs[2:]
    near, refs = refs[:13], refs[13:]
    state, lam, mu, buoy, residual, tiles, cells, resample, patch, fault_cell, area, moment, order = near
    (
        packed,
        landed,
        middle,
        arrived,
        source,
        onehot_hi,
        picks,
        sums_out,
        sums_in,
        x_out,
        x_low,
        x_high,
        y_out,
        y_low,
        y_high,
        fetch_sem,
        dip_send,
        dip_recv,
        strike_send,
        strike_recv,
        sum_send,
        sum_recv,
        halo_send,
        halo_recv,
    ) = refs
    count = strike_count * dip_count
    strike = lax.axis_index("strike")
    dip = lax.axis_index("dip")
    me = strike * dip_count + dip
    size_x, size_y, size_z = buoy.shape
    rows = size_x * size_y
    stations = residual.shape[1]
    steps = resample.shape[0]
    shift = size_z.bit_length() - 1
    width = packed.shape[2]
    slots = strike_count * LANES
    owned = order.shape[1] // count
    per_block = LANES // owned
    blocks = order.shape[1] // LANES

    def peer(k):
        to = lax.rem(me + k, count)
        return to, (to // dip_count, lax.rem(to, dip_count))

    barrier = pltpu.get_barrier_semaphore()

    def dip_peer(k):
        to = lax.rem(dip + k, dip_count)
        return to, (strike, to)

    def strike_peer(k):
        to = lax.rem(strike + k, strike_count)
        return to, (to, dip)

    def greet(which):
        def one(k, carry):
            pl.semaphore_signal(barrier, inc=1, device_id=which(k)[1], device_id_type=MESH)
            return carry

        return one

    lax.fori_loop(1, dip_count, greet(dip_peer), 0)
    lax.fori_loop(1, strike_count, greet(strike_peer), 0)

    fetches = [pltpu.make_async_copy(far[i], near[i], fetch_sem.at[i]) for i in range(13)]
    early = (5, 6, 7, 4)
    for i in early:
        fetches[i].start()
    for i in range(13):
        if i not in early:
            fetches[i].start()

    sides = (
        (strike > 0, (strike - 1, dip)),
        (strike < strike_count - 1, (strike + 1, dip)),
        (dip > 0, (strike, dip - 1)),
        (dip < dip_count - 1, (strike, dip + 1)),
    )
    halves = ((x_out, x_low, x_high), (y_out, y_low, y_high))

    def halo_copies(turn):
        copies = []
        for side in range(4):
            sender, low, high = halves[side // 2]
            target = high if side % 2 == 0 else low
            arrival = side ^ 1
            copies.append(
                pltpu.make_async_remote_copy(
                    src_ref=sender.at[turn, side % 2],
                    dst_ref=target.at[turn],
                    send_sem=halo_send.at[turn, side],
                    recv_sem=halo_recv.at[turn, arrival],
                    device_id=sides[side][1],
                    device_id_type=MESH,
                )
            )
        return copies

    def stage(turn, x_fields, y_fields):
        for c in range(3):
            f = out[x_fields[c]] if turn else state[x_fields[c]]
            x_out[turn, 0, c] = f[0]
            x_out[turn, 1, c] = f[size_x - 1]
            f = out[y_fields[c]] if turn else state[y_fields[c]]
            y_out[turn, 0, c] = f[:, 0:1]
            y_out[turn, 1, c] = f[:, size_y - 1 : size_y]

    def send(turn):
        for side, copy in enumerate(halo_copies(turn)):
            pl.when(sides[side][0])(copy.start)

    def receive(turn):
        for side, copy in enumerate(halo_copies(turn)):

            def finish(turn=turn, side=side, copy=copy):
                copy.wait_send()
                sender, low, high = halves[side // 2]
                target = low if side % 2 == 0 else high
                pltpu.make_async_copy(target.at[turn], target.at[turn], halo_recv.at[turn, side]).wait()

            pl.when(sides[side][0])(finish)

    for side in range(4):

        def clear(side=side):
            _, low, high = halves[side // 2]
            target = low if side % 2 == 0 else high
            target[...] = jnp.zeros_like(target)

        pl.when(jnp.logical_not(sides[side][0]))(clear)

    stress_x, stress_y = (3, 6, 7), (6, 4, 8)
    for i in early:
        fetches[i].wait()

    res_hi, res_lo = split(resample[...])
    weights = jnp.concatenate([res_hi, res_lo], axis=0)
    parts = [matmul_nt(weights, residual[c]) for c in range(3)]
    amplitude = [parts[c][k : k + 1] + parts[c][steps + k : steps + k + 1] for k in range(steps) for c in range(3)]
    cell_row = cells[...]
    hi_row = lax.shift_right_logical(cell_row, shift).astype(jnp.float32)
    lo_row = (cell_row & (size_z - 1)).astype(jnp.float32)
    values = jnp.concatenate(amplitude + [hi_row, lo_row], axis=0)
    tile_row = tiles[...]
    named = one_hot((count, stations), 0, tile_row)
    earlier = jnp.where(
        lax.broadcasted_iota(jnp.int32, (stations, stations), 0) < lax.broadcasted_iota(jnp.int32, (stations, stations), 1),
        1.0,
        0.0,
    ).astype(jnp.bfloat16)
    ordinal = jnp.sum(named.astype(jnp.float32) * matmul(named, earlier), axis=0, keepdims=True)
    slot_row = lax.rem(tile_row, dip_count) * width + (tile_row // dip_count) * slot_count + ordinal.astype(jnp.int32)
    placing = one_hot((dip_count * width, stations), 0, slot_row)
    val_hi, val_lo = split(values)
    placed = matmul_nt(jnp.concatenate([val_hi, val_lo], axis=0), placing)
    placed = placed[:8] + placed[8:]
    for p in range(dip_count):
        packed[p] = placed[:, p * width : (p + 1) * width]
    fetches[0].wait()
    stage(0, stress_x, stress_y)

    pl.semaphore_wait(barrier, dip_count + strike_count - 2)

    def route_dip(k, carry):
        to, device = dip_peer(k)
        pltpu.make_async_remote_copy(
            src_ref=packed.at[to],
            dst_ref=landed.at[dip],
            send_sem=dip_send,
            recv_sem=dip_recv,
            device_id=device,
            device_id_type=MESH,
        ).start()
        return carry

    lax.fori_loop(1, dip_count, route_dip, 0)
    send(0)
    landed[dip] = packed[dip]
    for i in range(1, 13):
        if i not in early:
            fetches[i].wait()

    patch_row = patch[...]
    entries = patch_row.shape[1]
    cell_e = fault_cell[...]
    pick_lo = one_hot((size_z, entries), 0, cell_e & (size_z - 1))
    onehot_hi[...] = jnp.where(
        lax.broadcasted_iota(jnp.int32, (rows, entries), 0) == lax.shift_right_logical(cell_e, shift), 1.0, 0.0
    )
    mom_hi, mom_lo = split(moment[...])
    chosen = matmul(jnp.concatenate([mom_hi, mom_lo], axis=0), one_hot((moment.shape[1], entries), 0, patch_row))
    pattern = (chosen[:6] + chosen[6:]) * area[...]
    patch_col = jnp.transpose(jnp.broadcast_to(patch_row.astype(jnp.float32), (LANES, entries)))
    for b in range(blocks):
        ids = order[:, b * LANES : (b + 1) * LANES].astype(jnp.float32)
        picks[:, b * LANES : (b + 1) * LANES] = jnp.where(patch_col == ids, 1.0, 0.0).astype(jnp.bfloat16)

    def force(turn, c, fields):
        xx, yy, zz = fields
        fx = (out if turn else state)[xx]
        fy = (out if turn else state)[yy]
        fz = (out if turn else state)[zz]
        total = along_x(fx, x_low[turn, c], x_high[turn, c]) + along_y(fy, y_low[turn, c], y_high[turn, c]) + along_z(fz)
        return time_step * (buoy[...] * total)

    rhs = ((3, 6, 7), (6, 4, 8), (7, 8, 5))

    def velocity(turn, step):
        for c in range(3):
            old = (out if turn else state)[c]
            moved = old + force(turn, c, rhs[c])
            if step:
                moved = moved + source[(step - 1) * 3 + c].reshape(size_x, size_y, size_z)
            out[c] = moved

    def stress(turn, first):
        old = state if first else out
        lam_v, mu_v = lam[...], mu[...]
        vx, vy, vz = out[0], out[1], out[2]
        dxx = along_x(vx, x_low[turn, 0], x_high[turn, 0])
        dyy = along_y(vy, y_low[turn, 1], y_high[turn, 1])
        dzz = along_z(vz)
        bulk = lam_v * (dxx + dyy + dzz)
        out[3] = old[3] + time_step * (bulk + 2.0 * mu_v * dxx)
        out[4] = old[4] + time_step * (bulk + 2.0 * mu_v * dyy)
        out[5] = old[5] + time_step * (bulk + 2.0 * mu_v * dzz)
        scaled = time_step * mu_v
        out[6] = old[6] + scaled * (
            along_y(vx, y_low[turn, 0], y_high[turn, 0]) + along_x(vy, x_low[turn, 1], x_high[turn, 1])
        )
        out[7] = old[7] + scaled * (along_z(vx) + along_x(vz, x_low[turn, 2], x_high[turn, 2]))
        out[8] = old[8] + scaled * (along_z(vy) + along_y(vz, y_low[turn, 2], y_high[turn, 2]))

    def contribution():
        total = None
        for m in range(6):
            high, low = split(out[3 + m].reshape(rows, size_z))
            taken = (matmul(high, pick_lo) + matmul(low, pick_lo)) * pattern[m : m + 1]
            total = taken if total is None else total + taken
        return jnp.sum(total * onehot_hi[...], axis=0, keepdims=True)

    from_dip = landed.at[pl.ds(0, dip_count - 1)]
    pltpu.make_async_copy(from_dip, from_dip, dip_recv).wait()
    lane = lax.broadcasted_iota(jnp.int32, (8, LANES), 1) // slot_count
    for t in range(strike_count):
        block, offset = divmod(t * slot_count, LANES)
        total = jnp.zeros((8, LANES), jnp.float32)
        for j in range(dip_count):
            piece = landed[j, :, block * LANES : (block + 1) * LANES]
            turn = (j * slot_count - offset) % LANES
            total = jnp.where(lane == j, pltpu.roll(piece, turn, 1) if turn else piece, total)
        middle[t] = total

    def route_strike(k, carry):
        to, device = strike_peer(k)
        pltpu.make_async_remote_copy(
            src_ref=middle.at[to],
            dst_ref=arrived.at[strike],
            send_sem=strike_send,
            recv_sem=strike_recv,
            device_id=device,
            device_id_type=MESH,
        ).start()
        return carry

    lax.fori_loop(1, strike_count, route_strike, 0)
    arrived[strike] = middle[strike]
    pltpu.make_async_copy(from_dip, from_dip, dip_send).wait()

    receive(0)
    velocity(0, 0)

    from_strike = arrived.at[pl.ds(0, strike_count - 1)]
    pltpu.make_async_copy(from_strike, from_strike, strike_recv).wait()
    inbox = jnp.concatenate([arrived[g] for g in range(strike_count)], axis=1)
    hi_ids = inbox[6:7].astype(jnp.int32)
    lo_ids = inbox[7:8].astype(jnp.int32)
    spread_lo = one_hot((size_z, slots), 0, lo_ids)
    row_mask = lax.broadcasted_iota(jnp.int32, (rows, slots), 0) == hi_ids
    amp_hi, amp_lo = split(inbox)
    amp_hi, amp_lo = amp_hi.astype(jnp.float32), amp_lo.astype(jnp.float32)

    def injected(m):
        high = jnp.where(row_mask, amp_hi[m : m + 1], 0.0).astype(jnp.bfloat16)
        low = jnp.where(row_mask, amp_lo[m : m + 1], 0.0).astype(jnp.bfloat16)
        return time_step * (matmul_nt(high, spread_lo) + matmul_nt(low, spread_lo))

    for c in range(3):
        out[c] = out[c] + injected(c).reshape(size_x, size_y, size_z)

    flow = (0, 1, 2)
    contribs = []
    for step in range(steps):
        if step:
            receive(2 * step)
            velocity(2 * step, step)
        stage(2 * step + 1, flow, flow)
        send(2 * step + 1)
        if step == 0:
            for m in range(3, steps * 3):
                source[m - 3] = injected(m)
            pltpu.make_async_copy(from_strike, from_strike, strike_send).wait()
        receive(2 * step + 1)
        stress(2 * step + 1, step == 0)
        if step < steps - 1:
            stage(2 * step + 2, stress_x, stress_y)
            send(2 * step + 2)
        contribs.append(contribution())

    con_hi, con_lo = split(jnp.concatenate(contribs, axis=0))
    summed = matmul(jnp.concatenate([con_hi, con_lo], axis=0), picks[...])
    summed = summed[:steps] + summed[steps:]
    for b in range(blocks):
        sums_out[b] = summed[:, b * LANES : (b + 1) * LANES]

    def spread(k, carry):
        to, device = peer(k)
        pltpu.make_async_remote_copy(
            src_ref=sums_out.at[to // per_block],
            dst_ref=sums_in.at[me],
            send_sem=sum_send,
            recv_sem=sum_recv,
            device_id=device,
            device_id_type=MESH,
        ).start()
        return carry

    lax.fori_loop(1, count, spread, 0)
    sums_in[me] = sums_out[me // per_block]
    all_sums = sums_in.at[pl.ds(0, count - 1)]
    pltpu.make_async_copy(all_sums, all_sums, sum_recv).wait()
    pltpu.make_async_copy(all_sums, all_sums, sum_send).wait()
    final = jnp.sum(sums_in[...], axis=0)
    final = jnp.concatenate([final, jnp.zeros((8 - steps, LANES), jnp.float32)], axis=0)
    first = lax.rem(me, per_block) * owned
    slip[...] = pltpu.roll(final, lax.rem(LANES - first, LANES), 1)[:steps, :owned]


def shards(
    adjoint_state,
    lame_lambda,
    lame_mu,
    buoyancy,
    residual,
    receiver_tile,
    receiver_cell,
    resample,
    fault_patch,
    fault_cell,
    fault_area,
    moment,
    subpatch_order,
):
    strike_count = lax.axis_size("strike")
    dip_count = lax.axis_size("dip")
    count = strike_count * dip_count
    stations = residual.shape[0]
    slot_count = max(2, (2 * stations + count - 1) // count)
    steps = resample.shape[0]
    size_x, size_y, size_z = buoyancy.shape
    rows = size_x * size_y
    width = -(-strike_count * slot_count // LANES) * LANES
    assert dip_count * slot_count <= LANES
    entries = fault_patch.shape[1]
    patches = moment.shape[1]
    turns = 2 * steps
    anywhere = pl.BlockSpec(memory_space=pl.ANY)
    vmem = pl.BlockSpec(memory_space=pltpu.VMEM)
    f32, bf16 = jnp.float32, jnp.bfloat16
    operands = (
        adjoint_state,
        lame_lambda,
        lame_mu,
        buoyancy,
        jnp.swapaxes(residual, 0, 1),
        receiver_tile.reshape(1, stations),
        receiver_cell.reshape(1, stations),
        resample,
        fault_patch,
        fault_cell,
        fault_area,
        moment,
        subpatch_order.reshape(1, -1),
    )
    return pl.pallas_call(
        functools.partial(kernel, strike_count, dip_count, slot_count),
        out_shape=(
            pltpu.VMEM(adjoint_state.shape, f32),
            pltpu.VMEM((steps, patches // count), f32),
        ),
        in_specs=[anywhere] * 13,
        out_specs=(vmem, vmem),
        scratch_shapes=[
            *(pltpu.VMEM(a.shape, a.dtype) for a in operands),
            pltpu.VMEM((dip_count, 8, width), f32),
            pltpu.VMEM((dip_count, 8, width), f32),
            pltpu.VMEM((strike_count, 8, LANES), f32),
            pltpu.VMEM((strike_count, 8, LANES), f32),
            pltpu.VMEM((steps * 3 - 3, rows, size_z), f32),
            pltpu.VMEM((rows, entries), f32),
            pltpu.VMEM((entries, patches), bf16),
            pltpu.VMEM((patches // LANES, steps, LANES), f32),
            pltpu.VMEM((count, steps, LANES), f32),
            pltpu.VMEM((turns, 2, 3, size_y, size_z), f32),
            pltpu.VMEM((turns, 3, size_y, size_z), f32),
            pltpu.VMEM((turns, 3, size_y, size_z), f32),
            pltpu.VMEM((turns, 2, 3, size_x, 1, size_z), f32),
            pltpu.VMEM((turns, 3, size_x, 1, size_z), f32),
            pltpu.VMEM((turns, 3, size_x, 1, size_z), f32),
            pltpu.SemaphoreType.DMA((13,)),
            pltpu.SemaphoreType.DMA,
            pltpu.SemaphoreType.DMA,
            pltpu.SemaphoreType.DMA,
            pltpu.SemaphoreType.DMA,
            pltpu.SemaphoreType.DMA,
            pltpu.SemaphoreType.DMA,
            pltpu.SemaphoreType.DMA((turns, 4)),
            pltpu.SemaphoreType.DMA((turns, 4)),
        ],
        compiler_params=pltpu.CompilerParams(collective_id=0, has_side_effects=True),
        name="adjoint",
    )(*operands)


def solution(mesh):
    return jax.shard_map(
        shards,
        mesh=mesh,
        in_specs=(
            P(None, "strike", "dip", None),
            P("strike", "dip", None),
            P("strike", "dip", None),
            P("strike", "dip", None),
            P(("strike", "dip"), None, None),
            P(("strike", "dip"), None),
            P(("strike", "dip")),
            P(),
            P(("strike", "dip"), None),
            P(("strike", "dip"), None),
            P(("strike", "dip"), None),
            P(),
            P(),
        ),
        out_specs=(P(None, "strike", "dip", None), P(None, ("strike", "dip"))),
        check_vma=False,
    )
```

```python
import functools

import jax
import jax.numpy as jnp
from jax import lax
from jax.experimental import pallas as pl
from jax.experimental.pallas import tpu as pltpu
from jax.sharding import PartitionSpec as P

STEPS = 2
LANES = 128

time_step = 0.25

MESH = pl.DeviceIdType.MESH
NT_DIMS = (((1,), (1,)), ((), ()))


def split(x):
    high = x.astype(jnp.bfloat16)
    return high, (x - high.astype(jnp.float32)).astype(jnp.bfloat16)


def one_hot(shape, axis, ids):
    return jnp.where(lax.broadcasted_iota(jnp.int32, shape, axis) == ids, 1.0, 0.0).astype(jnp.bfloat16)


def matmul(a, b):
    return jnp.dot(a, b, preferred_element_type=jnp.float32)


def matmul_nt(a, b):
    return lax.dot_general(a, b, NT_DIMS, preferred_element_type=jnp.float32)


def along_x(f, low, high):
    before = jnp.concatenate([low[None], f[:-1]], axis=0)
    after = jnp.concatenate([f[1:], high[None]], axis=0)
    return (after - before) * 0.5


def along_y(f, low, high):
    size = f.shape[1]
    at = lax.broadcasted_iota(jnp.int32, f.shape, 1)
    before = jnp.where(at == 0, low, pltpu.roll(f, 1, 1))
    after = jnp.where(at == size - 1, high, pltpu.roll(f, size - 1, 1))
    return (after - before) * 0.5


def along_z(f):
    size = f.shape[2]
    at = lax.broadcasted_iota(jnp.int32, f.shape, 2)
    before = jnp.where(at == 0, 0.0, pltpu.roll(f, 1, 2))
    after = jnp.where(at == size - 1, 0.0, pltpu.roll(f, size - 1, 2))
    return (after - before) * 0.5


def kernel(strike_count, dip_count, slot_count, *refs):
    (far, refs) = (refs[:13], refs[13:])
    (out, slip), refs = refs[:2], refs[2:]
    near, refs = refs[:13], refs[13:]
    state, lam, mu, buoy, residual, tiles, cells, resample, patch, fault_cell, area, moment, order = near
    (
        packed,
        landed,
        middle,
        arrived,
        source,
        onehot_hi,
        picks,
        sums_out,
        sums_in,
        x_out,
        x_low,
        x_high,
        y_out,
        y_low,
        y_high,
        fetch_sem,
        dip_send,
        dip_recv,
        strike_send,
        strike_recv,
        sum_send,
        sum_recv,
        halo_send,
        halo_recv,
    ) = refs
    count = strike_count * dip_count
    strike = lax.axis_index("strike")
    dip = lax.axis_index("dip")
    me = strike * dip_count + dip
    size_x, size_y, size_z = buoy.shape
    rows = size_x * size_y
    stations = residual.shape[1]
    steps = resample.shape[0]
    shift = size_z.bit_length() - 1
    width = packed.shape[2]
    slots = strike_count * LANES
    owned = order.shape[1] // count
    per_block = LANES // owned
    blocks = order.shape[1] // LANES

    def peer(k):
        to = lax.rem(me + k, count)
        return to, (to // dip_count, lax.rem(to, dip_count))

    barrier = pltpu.get_barrier_semaphore()

    def dip_peer(k):
        to = lax.rem(dip + k, dip_count)
        return to, (strike, to)

    def strike_peer(k):
        to = lax.rem(strike + k, strike_count)
        return to, (to, dip)

    def greet(which):
        def one(k, carry):
            pl.semaphore_signal(barrier, inc=1, device_id=which(k)[1], device_id_type=MESH)
            return carry

        return one

    lax.fori_loop(1, dip_count, greet(dip_peer), 0)
    lax.fori_loop(1, strike_count, greet(strike_peer), 0)

    fetches = [pltpu.make_async_copy(far[i], near[i], fetch_sem.at[i]) for i in range(13)]
    early = (5, 6, 7, 4)
    for i in early:
        fetches[i].start()
    for i in range(13):
        if i not in early:
            fetches[i].start()

    sides = (
        (strike > 0, (strike - 1, dip)),
        (strike < strike_count - 1, (strike + 1, dip)),
        (dip > 0, (strike, dip - 1)),
        (dip < dip_count - 1, (strike, dip + 1)),
    )
    halves = ((x_out, x_low, x_high), (y_out, y_low, y_high))

    def halo_copies(turn):
        copies = []
        for side in range(4):
            sender, low, high = halves[side // 2]
            target = high if side % 2 == 0 else low
            arrival = side ^ 1
            copies.append(
                pltpu.make_async_remote_copy(
                    src_ref=sender.at[turn, side % 2],
                    dst_ref=target.at[turn],
                    send_sem=halo_send.at[turn, side],
                    recv_sem=halo_recv.at[turn, arrival],
                    device_id=sides[side][1],
                    device_id_type=MESH,
                )
            )
        return copies

    def stage(turn, x_fields, y_fields):
        for c in range(3):
            f = out[x_fields[c]] if turn else state[x_fields[c]]
            x_out[turn, 0, c] = f[0]
            x_out[turn, 1, c] = f[size_x - 1]
            f = out[y_fields[c]] if turn else state[y_fields[c]]
            y_out[turn, 0, c] = f[:, 0:1]
            y_out[turn, 1, c] = f[:, size_y - 1 : size_y]

    def send(turn):
        for side, copy in enumerate(halo_copies(turn)):
            pl.when(sides[side][0])(copy.start)

    def receive(turn):
        for side, copy in enumerate(halo_copies(turn)):

            def finish(turn=turn, side=side, copy=copy):
                sender, low, high = halves[side // 2]
                target = low if side % 2 == 0 else high
                pltpu.make_async_copy(target.at[turn], target.at[turn], halo_recv.at[turn, side]).wait()

            pl.when(sides[side][0])(finish)

    for side in range(4):

        def clear(side=side):
            _, low, high = halves[side // 2]
            target = low if side % 2 == 0 else high
            target[...] = jnp.zeros_like(target)

        pl.when(jnp.logical_not(sides[side][0]))(clear)

    stress_x, stress_y = (3, 6, 7), (6, 4, 8)
    for i in early:
        fetches[i].wait()

    res_hi, res_lo = split(resample[...])
    weights = jnp.concatenate([res_hi, res_lo], axis=0)
    parts = [matmul_nt(weights, residual[c]) for c in range(3)]
    amplitude = [parts[c][k : k + 1] + parts[c][steps + k : steps + k + 1] for k in range(steps) for c in range(3)]
    cell_row = cells[...]
    hi_row = lax.shift_right_logical(cell_row, shift).astype(jnp.float32)
    lo_row = (cell_row & (size_z - 1)).astype(jnp.float32)
    values = jnp.concatenate(amplitude + [hi_row, lo_row], axis=0)
    tile_row = tiles[...]
    named = one_hot((count, stations), 0, tile_row)
    earlier = jnp.where(
        lax.broadcasted_iota(jnp.int32, (stations, stations), 0) < lax.broadcasted_iota(jnp.int32, (stations, stations), 1),
        1.0,
        0.0,
    ).astype(jnp.bfloat16)
    ordinal = jnp.sum(named.astype(jnp.float32) * matmul(named, earlier), axis=0, keepdims=True)
    slot_row = lax.rem(tile_row, dip_count) * width + (tile_row // dip_count) * slot_count + ordinal.astype(jnp.int32)
    placing = one_hot((dip_count * width, stations), 0, slot_row)
    val_hi, val_lo = split(values)
    placed = matmul_nt(jnp.concatenate([val_hi, val_lo], axis=0), placing)
    placed = placed[:8] + placed[8:]
    for p in range(dip_count):
        packed[p] = placed[:, p * width : (p + 1) * width]
    fetches[0].wait()
    stage(0, stress_x, stress_y)

    pl.semaphore_wait(barrier, dip_count + strike_count - 2)

    def route_dip(k, carry):
        to, device = dip_peer(k)
        pltpu.make_async_remote_copy(
            src_ref=packed.at[to],
            dst_ref=landed.at[dip],
            send_sem=dip_send,
            recv_sem=dip_recv,
            device_id=device,
            device_id_type=MESH,
        ).start()
        return carry

    lax.fori_loop(1, dip_count, route_dip, 0)
    send(0)
    landed[dip] = packed[dip]
    for i in range(1, 13):
        if i not in early:
            fetches[i].wait()

    patch_row = patch[...]
    entries = patch_row.shape[1]
    cell_e = fault_cell[...]
    pick_lo = one_hot((size_z, entries), 0, cell_e & (size_z - 1))
    onehot_hi[...] = jnp.where(
        lax.broadcasted_iota(jnp.int32, (rows, entries), 0) == lax.shift_right_logical(cell_e, shift), 1.0, 0.0
    )
    mom_hi, mom_lo = split(moment[...])
    chosen = matmul(jnp.concatenate([mom_hi, mom_lo], axis=0), one_hot((moment.shape[1], entries), 0, patch_row))
    pattern = (chosen[:6] + chosen[6:]) * area[...]
    patch_col = jnp.transpose(jnp.broadcast_to(patch_row.astype(jnp.float32), (LANES, entries)))
    for b in range(blocks):
        ids = order[:, b * LANES : (b + 1) * LANES].astype(jnp.float32)
        picks[:, b * LANES : (b + 1) * LANES] = jnp.where(patch_col == ids, 1.0, 0.0).astype(jnp.bfloat16)

    def force(turn, c, fields):
        xx, yy, zz = fields
        fx = (out if turn else state)[xx]
        fy = (out if turn else state)[yy]
        fz = (out if turn else state)[zz]
        total = along_x(fx, x_low[turn, c], x_high[turn, c]) + along_y(fy, y_low[turn, c], y_high[turn, c]) + along_z(fz)
        return time_step * (buoy[...] * total)

    rhs = ((3, 6, 7), (6, 4, 8), (7, 8, 5))

    def velocity(turn, step):
        for c in range(3):
            old = (out if turn else state)[c]
            moved = old + force(turn, c, rhs[c])
            if step:
                moved = moved + source[(step - 1) * 3 + c].reshape(size_x, size_y, size_z)
            out[c] = moved

    def stress(turn, first):
        old = state if first else out
        lam_v, mu_v = lam[...], mu[...]
        vx, vy, vz = out[0], out[1], out[2]
        dxx = along_x(vx, x_low[turn, 0], x_high[turn, 0])
        dyy = along_y(vy, y_low[turn, 1], y_high[turn, 1])
        dzz = along_z(vz)
        bulk = lam_v * (dxx + dyy + dzz)
        out[3] = old[3] + time_step * (bulk + 2.0 * mu_v * dxx)
        out[4] = old[4] + time_step * (bulk + 2.0 * mu_v * dyy)
        out[5] = old[5] + time_step * (bulk + 2.0 * mu_v * dzz)
        scaled = time_step * mu_v
        out[6] = old[6] + scaled * (
            along_y(vx, y_low[turn, 0], y_high[turn, 0]) + along_x(vy, x_low[turn, 1], x_high[turn, 1])
        )
        out[7] = old[7] + scaled * (along_z(vx) + along_x(vz, x_low[turn, 2], x_high[turn, 2]))
        out[8] = old[8] + scaled * (along_z(vy) + along_y(vz, y_low[turn, 2], y_high[turn, 2]))

    def contribution():
        total = None
        for m in range(6):
            high, low = split(out[3 + m].reshape(rows, size_z))
            taken = (matmul(high, pick_lo) + matmul(low, pick_lo)) * pattern[m : m + 1]
            total = taken if total is None else total + taken
        return jnp.sum(total * onehot_hi[...], axis=0, keepdims=True)

    from_dip = landed.at[pl.ds(0, dip_count - 1)]
    pltpu.make_async_copy(from_dip, from_dip, dip_recv).wait()
    lane = lax.broadcasted_iota(jnp.int32, (8, LANES), 1) // slot_count
    for t in range(strike_count):
        block, offset = divmod(t * slot_count, LANES)
        total = jnp.zeros((8, LANES), jnp.float32)
        for j in range(dip_count):
            piece = landed[j, :, block * LANES : (block + 1) * LANES]
            turn = (j * slot_count - offset) % LANES
            total = jnp.where(lane == j, pltpu.roll(piece, turn, 1) if turn else piece, total)
        middle[t] = total

    def route_strike(k, carry):
        to, device = strike_peer(k)
        pltpu.make_async_remote_copy(
            src_ref=middle.at[to],
            dst_ref=arrived.at[strike],
            send_sem=strike_send,
            recv_sem=strike_recv,
            device_id=device,
            device_id_type=MESH,
        ).start()
        return carry

    lax.fori_loop(1, strike_count, route_strike, 0)
    arrived[strike] = middle[strike]
    receive(0)
    velocity(0, 0)

    from_strike = arrived.at[pl.ds(0, strike_count - 1)]
    pltpu.make_async_copy(from_strike, from_strike, strike_recv).wait()
    inbox = jnp.concatenate([arrived[g] for g in range(strike_count)], axis=1)
    hi_ids = inbox[6:7].astype(jnp.int32)
    lo_ids = inbox[7:8].astype(jnp.int32)
    spread_lo = one_hot((size_z, slots), 0, lo_ids)
    row_mask = lax.broadcasted_iota(jnp.int32, (rows, slots), 0) == hi_ids
    amp_hi, amp_lo = split(inbox)
    amp_hi, amp_lo = amp_hi.astype(jnp.float32), amp_lo.astype(jnp.float32)

    def injected(m):
        high = jnp.where(row_mask, amp_hi[m : m + 1], 0.0).astype(jnp.bfloat16)
        low = jnp.where(row_mask, amp_lo[m : m + 1], 0.0).astype(jnp.bfloat16)
        return time_step * (matmul_nt(high, spread_lo) + matmul_nt(low, spread_lo))

    for c in range(3):
        out[c] = out[c] + injected(c).reshape(size_x, size_y, size_z)

    flow = (0, 1, 2)
    contribs = []
    for step in range(steps):
        if step:
            receive(2 * step)
            velocity(2 * step, step)
        stage(2 * step + 1, flow, flow)
        send(2 * step + 1)
        if step == 0:
            for m in range(3, steps * 3):
                source[m - 3] = injected(m)
        receive(2 * step + 1)
        stress(2 * step + 1, step == 0)
        if step < steps - 1:
            stage(2 * step + 2, stress_x, stress_y)
            send(2 * step + 2)
        contribs.append(contribution())

    con_hi, con_lo = split(jnp.concatenate(contribs, axis=0))
    summed = matmul(jnp.concatenate([con_hi, con_lo], axis=0), picks[...])
    summed = summed[:steps] + summed[steps:]
    for b in range(blocks):
        sums_out[b] = summed[:, b * LANES : (b + 1) * LANES]

    def spread(k, carry):
        to, device = peer(k)
        pltpu.make_async_remote_copy(
            src_ref=sums_out.at[to // per_block],
            dst_ref=sums_in.at[me],
            send_sem=sum_send,
            recv_sem=sum_recv,
            device_id=device,
            device_id_type=MESH,
        ).start()
        return carry

    lax.fori_loop(1, count, spread, 0)
    sums_in[me] = sums_out[me // per_block]
    all_sums = sums_in.at[pl.ds(0, count - 1)]
    pltpu.make_async_copy(all_sums, all_sums, sum_recv).wait()
    final = jnp.sum(sums_in[...], axis=0)
    final = jnp.concatenate([final, jnp.zeros((8 - steps, LANES), jnp.float32)], axis=0)
    first = lax.rem(me, per_block) * owned
    slip[...] = pltpu.roll(final, lax.rem(LANES - first, LANES), 1)[:steps, :owned]

    pltpu.make_async_copy(from_dip, from_dip, dip_send).wait()
    pltpu.make_async_copy(from_strike, from_strike, strike_send).wait()
    pltpu.make_async_copy(all_sums, all_sums, sum_send).wait()
    for turn in range(2 * steps):
        for side, copy in enumerate(halo_copies(turn)):
            pl.when(sides[side][0])(copy.wait_send)


def put(state, slip, out, grad, sems):
    copies = [pltpu.make_async_copy(state, out, sems.at[0]), pltpu.make_async_copy(slip, grad, sems.at[1])]
    for copy in copies:
        copy.start()
    for copy in copies:
        copy.wait()


def shards(
    adjoint_state,
    lame_lambda,
    lame_mu,
    buoyancy,
    residual,
    receiver_tile,
    receiver_cell,
    resample,
    fault_patch,
    fault_cell,
    fault_area,
    moment,
    subpatch_order,
):
    strike_count = lax.axis_size("strike")
    dip_count = lax.axis_size("dip")
    count = strike_count * dip_count
    stations = residual.shape[0]
    slot_count = max(2, (2 * stations + count - 1) // count)
    steps = resample.shape[0]
    size_x, size_y, size_z = buoyancy.shape
    rows = size_x * size_y
    width = -(-strike_count * slot_count // LANES) * LANES
    assert dip_count * slot_count <= LANES
    entries = fault_patch.shape[1]
    patches = moment.shape[1]
    turns = 2 * steps
    anywhere = pl.BlockSpec(memory_space=pl.ANY)
    vmem = pl.BlockSpec(memory_space=pltpu.VMEM)
    f32, bf16 = jnp.float32, jnp.bfloat16
    operands = (
        adjoint_state,
        lame_lambda,
        lame_mu,
        buoyancy,
        jnp.swapaxes(residual, 0, 1),
        receiver_tile.reshape(1, stations),
        receiver_cell.reshape(1, stations),
        resample,
        fault_patch,
        fault_cell,
        fault_area,
        moment,
        subpatch_order.reshape(1, -1),
    )
    state, slip = pl.pallas_call(
        functools.partial(kernel, strike_count, dip_count, slot_count),
        out_shape=(
            pltpu.VMEM(adjoint_state.shape, f32),
            pltpu.VMEM((steps, patches // count), f32),
        ),
        in_specs=[anywhere] * 13,
        out_specs=(vmem, vmem),
        scratch_shapes=[
            *(pltpu.VMEM(a.shape, a.dtype) for a in operands),
            pltpu.VMEM((dip_count, 8, width), f32),
            pltpu.VMEM((dip_count, 8, width), f32),
            pltpu.VMEM((strike_count, 8, LANES), f32),
            pltpu.VMEM((strike_count, 8, LANES), f32),
            pltpu.VMEM((steps * 3 - 3, rows, size_z), f32),
            pltpu.VMEM((rows, entries), f32),
            pltpu.VMEM((entries, patches), bf16),
            pltpu.VMEM((patches // LANES, steps, LANES), f32),
            pltpu.VMEM((count, steps, LANES), f32),
            pltpu.VMEM((turns, 2, 3, size_y, size_z), f32),
            pltpu.VMEM((turns, 3, size_y, size_z), f32),
            pltpu.VMEM((turns, 3, size_y, size_z), f32),
            pltpu.VMEM((turns, 2, 3, size_x, 1, size_z), f32),
            pltpu.VMEM((turns, 3, size_x, 1, size_z), f32),
            pltpu.VMEM((turns, 3, size_x, 1, size_z), f32),
            pltpu.SemaphoreType.DMA((13,)),
            pltpu.SemaphoreType.DMA,
            pltpu.SemaphoreType.DMA,
            pltpu.SemaphoreType.DMA,
            pltpu.SemaphoreType.DMA,
            pltpu.SemaphoreType.DMA,
            pltpu.SemaphoreType.DMA,
            pltpu.SemaphoreType.DMA((turns, 4)),
            pltpu.SemaphoreType.DMA((turns, 4)),
        ],
        compiler_params=pltpu.CompilerParams(collective_id=0, has_side_effects=True),
        name="adjoint",
    )(*operands)
    state = pltpu.with_memory_space_constraint(state, pltpu.VMEM)
    slip = pltpu.with_memory_space_constraint(slip, pltpu.VMEM)
    return pl.pallas_call(
        put,
        out_shape=(
            jax.ShapeDtypeStruct(state.shape, f32),
            jax.ShapeDtypeStruct(slip.shape, f32),
        ),
        in_specs=[vmem, vmem],
        out_specs=(anywhere, anywhere),
        scratch_shapes=[pltpu.SemaphoreType.DMA((2,))],
        name="put",
    )(state, slip)


def solution(mesh):
    return jax.shard_map(
        shards,
        mesh=mesh,
        in_specs=(
            P(None, "strike", "dip", None),
            P("strike", "dip", None),
            P("strike", "dip", None),
            P("strike", "dip", None),
            P(("strike", "dip"), None, None),
            P(("strike", "dip"), None),
            P(("strike", "dip")),
            P(),
            P(("strike", "dip"), None),
            P(("strike", "dip"), None),
            P(("strike", "dip"), None),
            P(),
            P(),
        ),
        out_specs=(P(None, "strike", "dip", None), P(None, ("strike", "dip"))),
        check_vma=False,
    )
```
